32 devices in a mesh: dp: 8 (over z, y), expert: 4 (over x, core).
Axes of the slice: x: 2, y: 2, z: 4, core: 2. Of those that a mesh axis runs over, the one named last changes fastest.
Arguments:
- tokens: bfloat16 [1024, 4096], P('dp'), may hold values from -6 to 6
- upstream: bfloat16 [1024, 4096], P('dp', 'expert'), may hold values from -6 to 6
- gates: bfloat16 [1024, 2], P('dp'), may hold values from 0.049804688 to 1
- expert_ids: int32 [1024, 2], P('dp'), may hold values from 0 to 7, all different within a row; in each aligned block of 128 rows (0 to 127, 128 to 255, ...) at most 64 rows name the same one
- w_gate: bfloat16 [8, 1536, 4096], P('dp', 'expert'), may hold values from -0.09375 to 0.09375
- w_up: bfloat16 [8, 1536, 4096], P('dp', 'expert'), may hold values from -0.09375 to 0.09375
- w_down: bfloat16 [8, 1536, 4096], P('dp', 'expert'), may hold values from -0.15625 to 0.15625
Outputs:
- grad_x: bfloat16 [1024, 4096], P('dp', 'expert')
- grad_gates: float32 [1024, 2], P('dp')
- grad_w_gate: bfloat16 [8, 1536, 4096], P('dp', 'expert')
- grad_w_up: bfloat16 [8, 1536, 4096], P('dp', 'expert')
- grad_w_down: bfloat16 [8, 1536, 4096], P('dp', 'expert')
The draws below stay inside these ranges and needn't reach their ends.
Inputs may be any that keep to these rules, and one draw needn't show every extreme that they name: `expert_ids`: each row names 2 different experts. In each aligned block of 128 rows (the tokens of one index of dp) no expert is named by more than 64 rows, a bound that some block reaches.
All inputs are finite; a program needn't handle non-finite values.
Results may differ from the reference program's by a relative error of at most 0.012.
Values may be sent and summed in bfloat16 or wider, within the bound.
A program may use at most 128 MiB of HBM per device.

```python
import math
import jax
import jax.numpy as jnp
import numpy as np
from jax import lax

D = 4096
HID = 1536
TOK_DEV = 128
TOP = 2
EXPERTS = 8
CAP = 64
TOKENS = 1024
N_DP = 8
N_EXPERT = 4


def shard_levels(stream_key, extent, pieces, low, top_value):
    def one(dim, blocks):
        steps = jax.random.uniform(jax.random.fold_in(jax.random.fold_in(stream_key, 6), dim), (blocks,), jnp.float32, low / len(pieces), top_value / len(pieces))
        return jnp.repeat(jnp.exp(steps), extent[dim] // blocks).reshape((-1,) + (1,) * (len(extent) - dim - 1))

    level = one(*pieces[0])
    for cut in pieces[1:]:
        level = level * one(*cut)
    return level


def shared_out(key, own, number, rows, number_of, top, bound, lean):
    ranking = jax.random.permutation(key, number_of)
    crowded, usual = shares(number_of, rows * top, bound, lean, True), shares(number_of, rows * top, bound, lean, False)
    places = jnp.arange(number_of)

    def named(lengths, turn):
        used = int((lengths > 0).sum())
        fixed = max(1, used // 4)
        moved = fixed + (places - fixed + turn * (used - fixed)) % max(1, number_of - fixed)
        return jnp.zeros((number_of,), jnp.int32).at[ranking[jnp.where(places < fixed, places, moved)]].set(jnp.asarray(lengths, jnp.int32))

    lengths = jnp.where(number % 4 == 0, named(crowded, number // 4), named(usual, number - number // 4 - 1))
    mixed = jax.random.permutation(jax.random.fold_in(own, 3), number_of)
    donor, taker = mixed[0:number_of // 2 * 2:2], mixed[1:number_of // 2 * 2:2]
    margin = jnp.minimum(lengths[donor] - 1, bound - lengths[taker]) // 2
    margin = jnp.where((donor == ranking[0]) | (taker == ranking[0]) | (lengths[taker] == 0), 0, jnp.maximum(margin, 0))
    moved = jax.random.randint(jax.random.fold_in(own, 4), (number_of // 2,), 0, 1 << 20) % (margin + 1)
    lengths = lengths.at[donor].add(-moved).at[taker].add(moved)
    members = jnp.searchsorted(jnp.cumsum(lengths), jnp.arange(rows * top), side="right").astype(jnp.int32)
    table = members.reshape(top, rows).T
    table = table[jax.random.permutation(jax.random.fold_in(own, 1), rows)]
    turn = jax.random.randint(jax.random.fold_in(own, 2), (rows, 1), 0, top)
    return jnp.take_along_axis(table, (jnp.arange(top)[None, :] + turn) % top, axis=1)


def shares(number_of, total, most, skew, full):
    weights = [(1 << 20) // math.isqrt(rank ** skew) + 1 for rank in range(1, number_of + 1)]
    largest = most if full else min(most, max(-(-total // number_of), total * weights[0] // sum(weights)))
    least = 1 if total - largest >= number_of - 1 else 0
    holding, rest = [largest] + [least] * (number_of - 1), total - largest - least * (number_of - 1)
    while rest > 0:
        free = [i for i in range(1, number_of) if holding[i] < largest] or [i for i in range(1, number_of) if holding[i] < most]
        mass, left = sum([weights[i] for i in free]), rest
        for i in free:
            more = min(most - holding[i], max(1, left * weights[i] // mass), rest)
            holding[i] = holding[i] + more
            rest = rest - more
    return np.array(holding)


def noise(stream_key, dims, scale, reach, split=(), kind=jnp.bfloat16):
    values = scale * jax.random.normal(stream_key, dims, jnp.float32)
    if split:
        values = values * shard_levels(stream_key, dims, split, -0.22, 0.18)
    return jnp.clip(values, -reach, reach).astype(kind)


def setup_inputs(seed: int = 0) -> dict:
    splits = jax.random.split(jax.random.key(seed), 8)
    tokens = noise(splits[0], (TOKENS, D), 1.0, 6.0, ((0, 8),))
    upstream = noise(splits[1], (TOKENS, D), 1.0, 6.0, ((0, 8), (1, 4)))
    gates = jnp.clip(jnp.exp(math.log(1.0) - 2.9996462 * jax.random.uniform(splits[2], (TOKENS, TOP), jnp.float32) ** shard_levels(splits[2], (TOKENS, TOP), ((0, 8),), -0.2, 0.2)), 0.049804688, 1.0).astype(jnp.bfloat16)
    expert_ids_keys = jax.random.split(jax.random.fold_in(splits[3], 1), TOKENS // TOK_DEV)
    expert_ids_turns = jax.random.permutation(jax.random.fold_in(splits[3], 3), TOKENS // TOK_DEV)
    expert_ids = jax.vmap(lambda own, number: shared_out(jax.random.fold_in(splits[3], 2), own, number, TOK_DEV, EXPERTS, TOP, CAP, 2))(expert_ids_keys, expert_ids_turns).reshape((TOKENS, TOP))
    w_gate = noise(splits[4], (EXPERTS, HID, D), D ** -0.5, 0.09375, ((0, 8), (1, 4)))
    w_up = noise(splits[5], (EXPERTS, HID, D), D ** -0.5, 0.09375, ((0, 8), (1, 4)))
    w_down = noise(splits[6], (EXPERTS, HID, D), HID ** -0.5, 0.15625, ((0, 8), (1, 4)))
    return dict(tokens=tokens, upstream=upstream, gates=gates, expert_ids=expert_ids, w_gate=w_gate, w_up=w_up, w_down=w_down)


def swish_pair(pre):
    sigma = jax.nn.sigmoid(pre)
    return pre * sigma, sigma * (1.0 + pre * (1.0 - sigma))


def contract_last(left, right):
    return lax.dot_general(left, right, (((1,), (1,)), ((), ())), preferred_element_type=jnp.float32)


def contract_first(left, right):
    return lax.dot_general(left, right, (((0,), (0,)), ((), ())), preferred_element_type=jnp.float32)


def reference(tokens, upstream, gates, expert_ids, w_gate, w_up, w_down):
    experts = w_gate.shape[0]
    hidden = w_gate.shape[1]
    width = tokens.shape[1]
    top = expert_ids.shape[1]
    groups = N_DP
    windows = N_EXPERT
    window = hidden // windows
    tok_rows = tokens.shape[0] // groups
    cap = 2 * tok_rows * top // experts
    rows = groups * cap
    block_ids = expert_ids.reshape(groups, tok_rows * top)
    onehot = (block_ids[:, :, None] == jnp.arange(experts, dtype=jnp.int32)[None, None, :]).astype(jnp.int32)
    position = jnp.sum((jnp.cumsum(onehot, axis=1) - onehot) * onehot, axis=2).astype(jnp.int32)
    blocks = jnp.arange(groups, dtype=jnp.int32)[:, None]
    slot = ((block_ids * groups + blocks) * cap + position).reshape(-1).astype(jnp.int32)
    count = slot.shape[0]
    owner = jnp.zeros((experts * rows,), jnp.int32).at[slot].set(jnp.arange(count, dtype=jnp.int32) + 1)
    owner = owner.reshape(experts, rows)
    flat_gates = gates.reshape(-1)

    def per_expert(packed):
        own, w_g, w_u, w_d = packed
        live = own > 0
        source = jnp.maximum(own - 1, 0)
        token_of = source // top
        inputs = jnp.where(live[:, None], tokens[token_of], jnp.zeros((), tokens.dtype))
        upward = jnp.where(live[:, None], upstream[token_of], jnp.zeros((), upstream.dtype))
        scales = jnp.where(live, flat_gates[source], jnp.zeros((), gates.dtype))
        pre_gate = contract_last(inputs, w_g)
        pre_up = contract_last(inputs, w_u)
        swish, slope = swish_pair(pre_gate)
        act = (swish * pre_up).astype(jnp.bfloat16)
        act_f = act.astype(jnp.float32)
        back = contract_last(upward, w_d)
        gate_term = jnp.sum(act_f * back, axis=1)
        scale_col = scales.astype(jnp.float32)[:, None]
        scaled = (scale_col * act_f).astype(jnp.bfloat16)
        grad_down = contract_first(scaled, upward).astype(jnp.bfloat16)
        weighted = scale_col * back
        d_gate = (weighted * pre_up * slope).astype(jnp.bfloat16)
        d_up = (weighted * swish).astype(jnp.bfloat16)
        grad_gate = contract_first(d_gate, inputs).astype(jnp.bfloat16)
        grad_up = contract_first(d_up, inputs).astype(jnp.bfloat16)
        total = jnp.zeros((rows, width), jnp.float32)
        for index in range(windows):
            low = index * window
            high = low + window
            piece = jnp.dot(d_gate[:, low:high], w_g[low:high], preferred_element_type=jnp.float32)
            piece = piece + jnp.dot(d_up[:, low:high], w_u[low:high], preferred_element_type=jnp.float32)
            piece = lax.optimization_barrier(piece.astype(jnp.bfloat16))
            total = total + piece.astype(jnp.float32)
        return total, gate_term, grad_gate, grad_up, grad_down

    totals, gate_terms, grad_w_gate, grad_w_up, grad_w_down = lax.map(per_expert, (owner, w_gate, w_up, w_down))
    totals = totals.reshape(experts * rows, width)
    gate_terms = gate_terms.reshape(-1)
    grad_x = jnp.sum(totals[slot].reshape(tokens.shape[0], top, width), axis=1).astype(jnp.bfloat16)
    grad_gates = gate_terms[slot].reshape(tokens.shape[0], top)
    return grad_x, grad_gates, grad_w_gate, grad_w_up, grad_w_down
```

```python
import jax
import jax.numpy as jnp
from jax import lax
from jax.sharding import PartitionSpec as P


def swish_pair(pre):
    sigma = jax.nn.sigmoid(pre)
    return (pre * sigma, sigma * (1.0 + pre * (1.0 - sigma)))


def contract_last(left, right):
    return lax.dot_general(
        left, right, (((1,), (1,)), ((), ())), preferred_element_type=jnp.float32
    )


def contract_first(left, right):
    return lax.dot_general(
        left, right, (((0,), (0,)), ((), ())), preferred_element_type=jnp.float32
    )


def expert_backward(inputs, upward, scale_col, w_g, w_u, w_d):
    pre_gate = contract_last(inputs, w_g)
    pre_up = contract_last(inputs, w_u)
    swish, slope = swish_pair(pre_gate)
    act = (swish * pre_up).astype(jnp.bfloat16)
    act_f = act.astype(jnp.float32)
    back = contract_last(upward, w_d)
    gate_term = jnp.sum(act_f * back, axis=1)
    scaled = (scale_col * act_f).astype(jnp.bfloat16)
    grad_down = contract_first(scaled, upward).astype(jnp.bfloat16)
    weighted = scale_col * back
    d_gate = (weighted * pre_up * slope).astype(jnp.bfloat16)
    d_up = (weighted * swish).astype(jnp.bfloat16)
    grad_gate = contract_first(d_gate, inputs).astype(jnp.bfloat16)
    grad_up = contract_first(d_up, inputs).astype(jnp.bfloat16)
    piece = jnp.dot(d_gate, w_g, preferred_element_type=jnp.float32)
    piece = piece + jnp.dot(d_up, w_u, preferred_element_type=jnp.float32)
    return (piece.astype(jnp.bfloat16), gate_term, grad_gate, grad_up, grad_down)


def per_device(tokens, upstream, gates, expert_ids, w_gate, w_up, w_down):
    groups = lax.axis_size("dp")
    experts = groups * w_gate.shape[0]
    tok_rows, width = tokens.shape
    top = expert_ids.shape[1]
    cap = 2 * tok_rows * top // experts
    part = upstream.shape[1]
    rows = experts * cap
    own = lax.axis_index("expert")
    tok_part = lax.dynamic_slice_in_dim(tokens, own * part, part, axis=1)
    flat = expert_ids.reshape(-1)
    count = flat.shape[0]
    earlier = jnp.arange(count)[None, :] < jnp.arange(count)[:, None]
    same = flat[:, None] == flat[None, :]
    position = jnp.sum((earlier & same).astype(jnp.int32), axis=1)
    slot = (flat * cap + position).reshape(tok_rows, top)
    hit = slot[None, :, :] == jnp.arange(rows, dtype=jnp.int32)[:, None, None]
    pick = jnp.sum(hit.astype(jnp.float32), axis=2).astype(jnp.bfloat16)
    scale = jnp.sum(jnp.where(hit, gates.astype(jnp.float32)[None], 0.0), axis=(1, 2))
    packed = jnp.concatenate([tok_part, upstream], axis=1)
    send = jnp.dot(pick, packed, preferred_element_type=jnp.float32).astype(jnp.bfloat16)
    send = jnp.concatenate(
        [send, jnp.broadcast_to(scale[:, None], (rows, 128)).astype(jnp.bfloat16)], axis=1
    )
    got = lax.all_to_all(send, "dp", split_axis=0, concat_axis=0, tiled=True)
    inputs = lax.all_gather(got[:, :part], "expert", axis=1, tiled=True)
    upward = lax.all_gather(got[:, part : 2 * part], "expert", axis=1, tiled=True)
    scale_col = got[:, 2 * part : 2 * part + 1].astype(jnp.float32)
    piece, term, grad_gate, grad_up, grad_down = expert_backward(
        inputs, upward, scale_col, w_gate[0], w_up[0], w_down[0]
    )
    total = lax.psum(term, "expert")
    summed = lax.psum_scatter(piece, "expert", scatter_dimension=1, tiled=True)
    high = total.astype(jnp.bfloat16)
    low = (total - high.astype(jnp.float32)).astype(jnp.bfloat16)
    lane = lax.broadcasted_iota(jnp.int32, (rows, 128), 1)
    tail = jnp.where(lane == 0, high[:, None], low[:, None])
    home = lax.all_to_all(
        jnp.concatenate([summed, tail], axis=1), "dp", split_axis=0, concat_axis=0, tiled=True
    )
    grad_x = contract_first(pick, home[:, :part]).astype(jnp.bfloat16)
    terms = home[:, part].astype(jnp.float32) + home[:, part + 1].astype(jnp.float32)
    grad_gates = jnp.sum(jnp.where(hit, terms[:, None, None], 0.0), axis=0)
    return (grad_x, grad_gates, grad_gate[None], grad_up[None], grad_down[None])


def solution(mesh):
    in_specs = (
        P("dp", None),
        P("dp", "expert"),
        P("dp", None),
        P("dp", None),
        P("dp", "expert", None),
        P("dp", "expert", None),
        P("dp", "expert", None),
    )
    out_specs = (
        P("dp", "expert"),
        P("dp", None),
        P("dp", "expert", None),
        P("dp", "expert", None),
        P("dp", "expert", None),
    )
    return jax.shard_map(
        per_device, mesh=mesh, in_specs=in_specs, out_specs=out_specs, check_vma=False
    )
```

```python
import functools

import jax
import jax.numpy as jnp
from jax import lax
from jax.experimental import pallas as pl
from jax.experimental.pallas import tpu as pltpu
from jax.sharding import PartitionSpec as P

MESH = pltpu.DeviceIdType.MESH if hasattr(pltpu, "DeviceIdType") else pl.DeviceIdType.MESH


def contract_last(left, right):
    return lax.dot_general(
        left, right, (((1,), (1,)), ((), ())), preferred_element_type=jnp.float32
    )


def contract_first(left, right):
    return lax.dot_general(
        left, right, (((0,), (0,)), ((), ())), preferred_element_type=jnp.float32
    )


def matmul(left, right):
    return jnp.dot(left, right, preferred_element_type=jnp.float32)


def kernel(
    groups, parts,
    send_t, send_u, send_s, w_g_hbm, w_u_hbm, w_d_hbm,
    home, home_s, out_g, out_u, out_d,
    recv_t, recv_u, recv_s, weights, pre, flipped, straight, grads,
    term, term_recv, total_term,
    pair_send, pair_recv, side_send, side_recv, own_sum, out_send,
    w_sem, g_sem, local_sem, recv_sem, scale_sem, dp_send, pair_fwd, side_fwd,
    scale_send, pair_send_sem, pair_recv_sem, side_send_sem, side_recv_sem,
    home_send, home_recv, term_send, term_sem, back_send, back_recv,
):
    me, own = lax.axis_index("dp"), lax.axis_index("expert")
    core, place = lax.rem(own, 2), lax.div(own, 2)
    places = parts // 2
    partner = place * 2 + (1 - core)
    cap, part = send_t.shape[1:]
    rows = groups * cap
    hid = weights.shape[2]
    sends, recvs = (send_t, send_u), (recv_t, recv_u)

    def ahead(k):
        return lax.rem(me + k, groups)

    def behind(k):
        return lax.rem(me + groups - k, groups)

    def aside(j):
        return lax.rem(place + j, places)

    def remote(src, dst, send_sem, sem, target):
        return pltpu.make_async_remote_copy(
            src_ref=src, dst_ref=dst, send_sem=send_sem, recv_sem=sem,
            device_id=target, device_id_type=MESH,
        )

    def arrived(ref, sem):
        pltpu.make_async_copy(ref, ref, sem).wait()

    loads = []
    for m, w_hbm in enumerate((w_g_hbm, w_u_hbm, w_d_hbm)):
        for j in range(parts):
            load = pltpu.make_async_copy(
                w_hbm.at[:, pl.ds(j * part, part)], weights.at[m, j], w_sem.at[m, j]
            )
            load.start()
            loads.append(load)

    barrier = pltpu.get_barrier_semaphore()
    for k in range(1, groups):
        pl.semaphore_signal(barrier, inc=1, device_id={"dp": ahead(k)}, device_id_type=MESH)
    for j in range(1, parts):
        pl.semaphore_signal(
            barrier, inc=1, device_id={"expert": lax.rem(own + j, parts)}, device_id_type=MESH
        )
    pl.semaphore_wait(barrier, groups + parts - 2)

    for k in range(1, groups):
        to = ahead(k)
        for t in range(2):
            if t == 0:
                remote(send_t.at[to], recv_t.at[own, me], dp_send.at[0],
                       recv_sem.at[0, own, me], {"dp": to}).start()
    for k in range(1, groups):
        to = ahead(k)
        remote(send_s.at[to], recv_s.at[me], scale_send, scale_sem.at[me], {"dp": to}).start()
        remote(send_u.at[to], recv_u.at[own, me], dp_send.at[1],
               recv_sem.at[1, own, me], {"dp": to}).start()
    keeps = []
    for t in range(2):
        keep = pltpu.make_async_copy(sends[t].at[me], recvs[t].at[own, me], local_sem.at[t])
        keep.start()
        keeps.append(keep)
    recv_s[me] = send_s[me]

    def relay(t, k):
        s = behind(k)
        spot = recvs[t].at[own, s]
        if k == 0:
            source = sends[t].at[me]
        else:
            arrived(spot, recv_sem.at[t, own, s])
            source = spot
        for j in range(1, places):
            remote(source, spot, side_fwd.at[t], recv_sem.at[t, own, s],
                   {"expert": aside(j) * 2 + core}).start()
        remote(source, spot, pair_fwd.at[t], recv_sem.at[t, own, s], {"expert": partner}).start()

    def pass_on(t, k):
        s = behind(k)
        for j in range(1, places):
            part_of = aside(j) * 2 + core
            spot = recvs[t].at[part_of, s]
            arrived(spot, recv_sem.at[t, part_of, s])
            remote(spot, spot, pair_fwd.at[t], recv_sem.at[t, part_of, s],
                   {"expert": partner}).start()

    def finish(t):
        keeps[t].wait()
        for k in range(groups):
            s = behind(k)
            for j in range(places):
                part_of = aside(j) * 2 + (1 - core)
                arrived(recvs[t].at[part_of, s], recv_sem.at[t, part_of, s])

    def forward_unit(m, j):
        loads[m * parts + j].wait()
        block = recvs[m // 2][j].reshape(rows, part)
        value = contract_last(weights[m, j], block)
        if j == 0:
            pre[m] = value
        else:
            pre[m] = pre[m] + value

    units = [(m, j) for m in range(2) for j in range(parts)]
    steps = [(t, k) for t in range(2) for k in range(groups)]
    lag = 2
    begin = groups + lag
    for i in range(len(steps) + lag):
        if i < len(steps):
            relay(*steps[i])
        if i >= lag:
            pass_on(*steps[i - lag])
        if i == begin - 1:
            finish(0)
        if i >= begin - 1:
            share = -(-len(units) // max(1, len(steps) + lag - i))
            for _ in range(share):
                if units:
                    forward_unit(*units.pop(0))
    for unit in units:
        forward_unit(*unit)
    finish(1)
    for j in range(parts):
        forward_unit(2, j)

    for k in range(1, groups):
        arrived(recv_s.at[behind(k)], scale_sem.at[behind(k)])
    scale = jnp.transpose(recv_s[...].reshape(rows, 128).astype(jnp.float32))[0:1, :]
    tile = 32
    term[...] = jnp.zeros_like(term)

    @pl.loop(0, hid // tile)
    def _(step):
        at = pl.ds(pl.multiple_of(step * tile, tile), tile)
        gate, up, back = pre[0, at, :], pre[1, at, :], pre[2, at, :]
        sigma = jax.nn.sigmoid(gate)
        swish = gate * sigma
        slope = sigma * (1.0 + gate * (1.0 - sigma))
        act = (swish * up).astype(jnp.bfloat16).astype(jnp.float32)
        term[...] += jnp.broadcast_to(jnp.sum(act * back, axis=0, keepdims=True), term.shape)
        weighted = scale * back
        flipped[0, at, :] = (weighted * up * slope).astype(jnp.bfloat16)
        flipped[1, at, :] = (weighted * swish).astype(jnp.bfloat16)
        flipped[2, at, :] = (scale * act).astype(jnp.bfloat16)

    for j in range(1, parts):
        remote(term, term_recv.at[own], term_send, term_sem.at[own],
               {"expert": lax.rem(own + j, parts)}).start()
    for m in range(2):
        straight[m] = jnp.transpose(flipped[m].astype(jnp.float32)).astype(jnp.bfloat16)

    block_rows = min(rows, 256)

    def piece(which, lo):
        at = pl.ds(lo, block_rows)
        value = matmul(straight[0, at, :], weights[0, which])
        return value + matmul(straight[1, at, :], weights[1, which])

    chunk = block_rows // cap
    for j in list(range(1, places)) + [0]:
        there = aside(j) * 2
        for lo in range(0, rows, block_rows):
            value = piece(there + 1 - core, lo).astype(jnp.bfloat16)
            pair_send[j, pl.ds(lo // cap, chunk)] = value.reshape(chunk, cap, part)
        pair = remote(pair_send.at[j], pair_recv.at[j], pair_send_sem.at[j],
                      pair_recv_sem.at[j], {"expert": partner})
        pair.start()
        for lo in range(0, rows, block_rows):
            value = piece(there + core, lo)
            own_sum[pl.ds(lo // cap, chunk)] = value.reshape(chunk, cap, part)
        pair.wait_recv()
        if j == 0:
            continue
        for k in list(range(1, groups)) + [0]:
            to = ahead(k)
            both = own_sum[to] + pair_recv[j, to].astype(jnp.float32)
            side_send[j, to] = both.astype(jnp.bfloat16)
            remote(side_send.at[j, to], side_recv.at[j, to], side_send_sem.at[j],
                   side_recv_sem.at[j, to], {"expert": there + core}).start()

    stores = []

    def grad_unit(m, j):
        block = recvs[m // 2][j].reshape(rows, part)
        grads[m, j] = matmul(flipped[m], block).astype(jnp.bfloat16)
        store = pltpu.make_async_copy(
            grads.at[m, j], (out_g, out_u, out_d)[m].at[:, pl.ds(j * part, part)], g_sem.at[m, j]
        )
        store.start()
        stores.append(store)

    for j in range(1, parts):
        arrived(term_recv.at[lax.rem(own + j, parts)], term_sem.at[lax.rem(own + j, parts)])
    term_recv[own] = term[...]
    total = term_recv[0]
    for j in range(1, parts):
        total = total + term_recv[j]
    total_term[...] = total
    home_s[me] = total
    for k in range(1, groups):
        remote(total_term, home_s.at[me], back_send, back_recv.at[me], {"dp": ahead(k)}).start()

    units = [(m, j) for m in range(3) for j in range(parts)]
    order = list(range(1, groups)) + [0]
    for i, k in enumerate(order):
        for _ in range(-(-len(units) // (len(order) - i))):
            grad_unit(*units.pop(0))
        to = ahead(k)
        value = own_sum[to] + pair_recv[0, to].astype(jnp.float32)
        for j in range(1, places):
            arrived(side_recv.at[j, to], side_recv_sem.at[j, to])
            value = value + side_recv[j, to].astype(jnp.float32)
        if k == 0:
            home[me] = value.astype(jnp.bfloat16)
        else:
            out_send[to] = value.astype(jnp.bfloat16)
            remote(out_send.at[to], home.at[me], home_send, home_recv.at[me], {"dp": to}).start()

    for k in range(1, groups):
        s = behind(k)
        arrived(home.at[s], home_recv.at[s])
        arrived(home_s.at[s], back_recv.at[s])
    for store in stores:
        store.wait()
    arrived(recv_s.at[pl.ds(0, groups - 1)], scale_send)
    arrived(home.at[pl.ds(0, groups - 1)], home_send)
    arrived(home_s.at[pl.ds(0, groups - 1)], back_send)
    arrived(term_recv.at[pl.ds(0, parts - 1)], term_send)
    for t in range(2):
        arrived(recvs[t].at[0, pl.ds(0, groups - 1)], dp_send.at[t])
        arrived(recvs[t].at[pl.ds(0, places)], pair_fwd.at[t])
        if places > 1:
            arrived(recvs[t].at[pl.ds(0, places - 1)], side_fwd.at[t])
    for j in range(places):
        arrived(pair_send.at[j], pair_send_sem.at[j])
        if j:
            arrived(side_send.at[j], side_send_sem.at[j])


def exchange(send_t, send_u, send_s, w_gate, w_up, w_down, parts):
    groups, cap, part = send_t.shape
    rows = groups * cap
    hid, width = w_gate.shape
    places = parts // 2
    bf, f32 = jnp.bfloat16, jnp.float32
    dma = pltpu.SemaphoreType.DMA
    vmem = pl.BlockSpec(memory_space=pltpu.VMEM)
    hbm = pl.BlockSpec(memory_space=pl.ANY)
    grad = jax.ShapeDtypeStruct((hid, width), bf)
    return pl.pallas_call(
        functools.partial(kernel, groups, parts),
        out_shape=(
            jax.ShapeDtypeStruct((groups, cap, part), bf),
            jax.ShapeDtypeStruct((groups, 8, rows), f32),
            grad, grad, grad,
        ),
        in_specs=[vmem] * 3 + [hbm] * 3,
        out_specs=(vmem, vmem, hbm, hbm, hbm),
        scratch_shapes=[
            pltpu.VMEM((parts, groups, cap, part), bf),
            pltpu.VMEM((parts, groups, cap, part), bf),
            pltpu.VMEM((groups, cap, 128), bf),
            pltpu.VMEM((3, parts, hid, part), bf),
            pltpu.VMEM((3, hid, rows), f32),
            pltpu.VMEM((3, hid, rows), bf),
            pltpu.VMEM((2, rows, hid), bf),
            pltpu.VMEM((3, parts, hid, part), bf),
            pltpu.VMEM((8, rows), f32),
            pltpu.VMEM((parts, 8, rows), f32),
            pltpu.VMEM((8, rows), f32),
            pltpu.VMEM((places, groups, cap, part), bf),
            pltpu.VMEM((places, groups, cap, part), bf),
            pltpu.VMEM((places, groups, cap, part), bf),
            pltpu.VMEM((places, groups, cap, part), bf),
            pltpu.VMEM((groups, cap, part), f32),
            pltpu.VMEM((groups, cap, part), bf),
            dma((3, parts)), dma((3, parts)), dma((2,)), dma((2, parts, groups)),
            dma((groups,)), dma((2,)), dma((2,)), dma((2,)), dma,
            dma((places,)), dma((places,)), dma((places,)), dma((places, groups)),
            dma, dma((groups,)), dma, dma((parts,)), dma, dma((groups,)),
        ],
        compiler_params=pltpu.CompilerParams(
            collective_id=0, has_side_effects=True, vmem_limit_bytes=62 * 1024 * 1024
        ),
    )(send_t, send_u, send_s, w_gate, w_up, w_down)


def per_device(tokens, upstream, gates, expert_ids, w_gate, w_up, w_down):
    groups = lax.axis_size("dp")
    parts = lax.axis_size("expert")
    experts = groups * w_gate.shape[0]
    tok_rows, width = tokens.shape
    top = expert_ids.shape[1]
    cap = 2 * tok_rows * top // experts
    part = upstream.shape[1]
    rows = experts * cap
    own = lax.axis_index("expert")
    tok_part = lax.dynamic_slice_in_dim(tokens, own * part, part, axis=1)
    flat = expert_ids.reshape(-1)
    count = flat.shape[0]
    earlier = jnp.arange(count)[None, :] < jnp.arange(count)[:, None]
    same = flat[:, None] == flat[None, :]
    position = jnp.sum((earlier & same).astype(jnp.int32), axis=1)
    slot = (flat * cap + position).reshape(tok_rows, top)
    hit = slot[None, :, :] == jnp.arange(rows, dtype=jnp.int32)[:, None, None]
    pick = jnp.sum(hit.astype(jnp.float32), axis=2).astype(jnp.bfloat16)
    scale = jnp.sum(jnp.where(hit, gates.astype(jnp.float32)[None], 0.0), axis=(1, 2))
    send_t = matmul(pick, tok_part).astype(jnp.bfloat16).reshape(groups, cap, part)
    send_u = matmul(pick, upstream).astype(jnp.bfloat16).reshape(groups, cap, part)
    send_s = jnp.broadcast_to(scale[:, None], (rows, 128)).astype(jnp.bfloat16)
    home, home_s, grad_gate, grad_up, grad_down = exchange(
        send_t, send_u, send_s.reshape(groups, cap, 128), w_gate[0], w_up[0], w_down[0], parts
    )
    grad_x = contract_first(pick, home.reshape(rows, part)).astype(jnp.bfloat16)
    terms = home_s[:, 0, :].reshape(groups, groups, cap)
    terms = lax.dynamic_index_in_dim(terms, lax.axis_index("dp"), 1, keepdims=False).reshape(rows)
    grad_gates = jnp.sum(jnp.where(hit, terms[:, None, None], 0.0), axis=0)
    return (grad_x, grad_gates, grad_gate[None], grad_up[None], grad_down[None])


def solution(mesh):
    in_specs = (
        P("dp", None),
        P("dp", "expert"),
        P("dp", None),
        P("dp", None),
        P("dp", "expert", None),
        P("dp", "expert", None),
        P("dp", "expert", None),
    )
    out_specs = (
        P("dp", "expert"),
        P("dp", None),
        P("dp", "expert", None),
        P("dp", "expert", None),
        P("dp", "expert", None),
    )
    return jax.shard_map(
        per_device, mesh=mesh, in_specs=in_specs, out_specs=out_specs, check_vma=False
    )
```

```python
import functools

import jax
import jax.numpy as jnp
from jax import lax
from jax.experimental import pallas as pl
from jax.experimental.pallas import tpu as pltpu
from jax.sharding import PartitionSpec as P

MESH = pltpu.DeviceIdType.MESH if hasattr(pltpu, "DeviceIdType") else pl.DeviceIdType.MESH


def contract_last(left, right):
    return lax.dot_general(
        left, right, (((1,), (1,)), ((), ())), preferred_element_type=jnp.float32
    )


def contract_first(left, right):
    return lax.dot_general(
        left, right, (((0,), (0,)), ((), ())), preferred_element_type=jnp.float32
    )


def matmul(left, right):
    return jnp.dot(left, right, preferred_element_type=jnp.float32)


def kernel(
    groups, parts,
    send_t, send_u, send_s, w_g_hbm, w_u_hbm, w_d_hbm,
    home, home_s, out_g, out_u, out_d,
    recv_t, recv_u, recv_s, weights, pre, flipped, straight, grads,
    term, term_recv, total_term,
    pair_send, pair_recv, side_send, side_recv, own_sum, out_send,
    w_sem, g_sem, local_sem, recv_sem, scale_sem, dp_send, pair_fwd, side_fwd,
    scale_send, pair_send_sem, pair_recv_sem, side_send_sem, side_recv_sem,
    home_send, home_recv, term_send, term_sem, back_send, back_recv,
):
    me, own = lax.axis_index("dp"), lax.axis_index("expert")
    core, place = lax.rem(own, 2), lax.div(own, 2)
    places = parts // 2
    partner = place * 2 + (1 - core)
    cap, part = send_t.shape[1:]
    rows = groups * cap
    hid = weights.shape[2]
    sends, recvs = (send_t, send_u), (recv_t, recv_u)

    half = groups // 2
    span = half * cap
    odds = [k for k in range(groups // 2 - 1, 0, -1) if k % 2]
    shifts = [0, groups // 2] + odds
    shifts = shifts + [k for k in range(groups) if k not in shifts]

    def ahead(p):
        return lax.rem(me + shifts[p], groups)

    def behind(p):
        return lax.rem(me + groups - shifts[p], groups)

    def aside(j):
        return lax.rem(place + j, places)

    def remote(src, dst, send_sem, sem, target):
        return pltpu.make_async_remote_copy(
            src_ref=src, dst_ref=dst, send_sem=send_sem, recv_sem=sem,
            device_id=target, device_id_type=MESH,
        )

    def arrived(ref, sem):
        pltpu.make_async_copy(ref, ref, sem).wait()

    barrier = pltpu.get_barrier_semaphore()
    for p in range(1, groups):
        pl.semaphore_signal(barrier, inc=1, device_id={"dp": ahead(p)}, device_id_type=MESH)
    for j in range(1, parts):
        pl.semaphore_signal(
            barrier, inc=1, device_id={"expert": lax.rem(own + j, parts)}, device_id_type=MESH
        )
    keeps = []
    for t in range(2):
        keep = pltpu.make_async_copy(sends[t].at[me], recvs[t].at[own, 0], local_sem.at[t])
        keep.start()
        keeps.append(keep)
    loads = []
    for m, w_hbm in enumerate((w_g_hbm, w_u_hbm, w_d_hbm)):
        for j in range(parts):
            load = pltpu.make_async_copy(
                w_hbm.at[:, pl.ds(j * part, part)], weights.at[m, j], w_sem.at[m, j]
            )
            load.start()
            loads.append(load)
    pl.semaphore_wait(barrier, groups + parts - 2)

    def halves(h):
        return range(h * half, (h + 1) * half)

    for h in range(2):
        for t in range(2):
            for p in halves(h):
                if p == 0:
                    continue
                to = ahead(p)
                remote(sends[t].at[to], recvs[t].at[own, p], dp_send.at[t],
                       recv_sem.at[t, own, p], {"dp": to}).start()
                if t == 0:
                    remote(send_s.at[to], recv_s.at[p], scale_send, scale_sem.at[p],
                           {"dp": to}).start()
    recv_s[0] = send_s[me]

    def relay(t, p):
        spot = recvs[t].at[own, p]
        if p == 0:
            source = sends[t].at[me]
        else:
            arrived(spot, recv_sem.at[t, own, p])
            source = spot
        for j in range(1, places):
            remote(source, spot, side_fwd.at[t], recv_sem.at[t, own, p],
                   {"expert": aside(j) * 2 + core}).start()
        remote(source, spot, pair_fwd.at[t], recv_sem.at[t, own, p], {"expert": partner}).start()

    def pass_on(t, p):
        for j in range(1, places):
            part_of = aside(j) * 2 + core
            spot = recvs[t].at[part_of, p]
            arrived(spot, recv_sem.at[t, part_of, p])
            remote(spot, spot, pair_fwd.at[t], recv_sem.at[t, part_of, p],
                   {"expert": partner}).start()

    def finish(t, h):
        if h == 0:
            keeps[t].wait()
        for p in halves(h):
            for j in range(places):
                part_of = aside(j) * 2 + (1 - core)
                arrived(recvs[t].at[part_of, p], recv_sem.at[t, part_of, p])

    def rows_of(t, j, h):
        return recvs[t][j, h * half : (h + 1) * half].reshape(span, part)

    def forward_unit(m, j, h):
        if h == 0:
            loads[m * parts + j].wait()
        value = contract_last(weights[m, j], rows_of(m // 2, j, h))
        if j == 0:
            pre[h, m] = value
        else:
            pre[h, m] = pre[h, m] + value

    tile = 32

    def middle(h):
        for p in halves(h):
            if p:
                arrived(recv_s.at[p], scale_sem.at[p])
        scale = recv_s[h * half : (h + 1) * half].reshape(span, 128).astype(jnp.float32)
        scale = jnp.transpose(scale)[0:1, :]
        term[h] = jnp.zeros(term.shape[1:], term.dtype)

        @pl.loop(0, hid // tile)
        def _(step):
            at = pl.ds(pl.multiple_of(step * tile, tile), tile)
            gate, up, back = pre[h, 0, at, :], pre[h, 1, at, :], pre[h, 2, at, :]
            sigma = jax.nn.sigmoid(gate)
            swish = gate * sigma
            slope = sigma * (1.0 + gate * (1.0 - sigma))
            act = (swish * up).astype(jnp.bfloat16).astype(jnp.float32)
            line = jnp.sum(act * back, axis=0, keepdims=True)
            term[h] += jnp.broadcast_to(line, term.shape[1:])
            weighted = scale * back
            flipped[h, 0, at, :] = (weighted * up * slope).astype(jnp.bfloat16)
            flipped[h, 1, at, :] = (weighted * swish).astype(jnp.bfloat16)
            flipped[h, 2, at, :] = (scale * act).astype(jnp.bfloat16)

    def turn(m, h):
        straight[h, m] = jnp.transpose(flipped[h, m].astype(jnp.float32)).astype(jnp.bfloat16)

    def piece(which, h):
        value = matmul(straight[h, 0], weights[0, which])
        value = value + matmul(straight[h, 1], weights[1, which])
        return value.reshape(half, cap, part)

    def to_pair(j, h):
        at = pl.ds(h * half, half)
        pair_send[j, at] = piece(aside(j) * 2 + 1 - core, h).astype(jnp.bfloat16)
        remote(pair_send.at[j, at], pair_recv.at[j, at], pair_send_sem.at[j],
               pair_recv_sem.at[j, h], {"expert": partner}).start()

    def to_side(j, h):
        at = pl.ds(h * half, half)
        value = piece(aside(j) * 2 + core, h)
        arrived(pair_recv.at[j, at], pair_recv_sem.at[j, h])
        value = value + pair_recv[j, at].astype(jnp.float32)
        if j == 0:
            own_sum[at] = value
            return
        side_send[j, at] = value.astype(jnp.bfloat16)
        for p in list(halves(h))[::-1]:
            remote(side_send.at[j, p], side_recv.at[j, p], side_send_sem.at[j],
                   side_recv_sem.at[j, p], {"expert": aside(j) * 2 + core}).start()

    def go_home(p):
        value = own_sum[p]
        for j in range(1, places):
            arrived(side_recv.at[j, p], side_recv_sem.at[j, p])
            value = value + side_recv[j, p].astype(jnp.float32)
        if p == 0:
            home[me] = value.astype(jnp.bfloat16)
        else:
            out_send[p] = value.astype(jnp.bfloat16)
            remote(out_send.at[p], home.at[me], home_send, home_recv.at[p],
                   {"dp": behind(p)}).start()

    call = functools.partial

    def first_tasks(h):
        jobs = [call(finish, 0, h)]
        return jobs + [call(forward_unit, m, j, h) for m in range(2) for j in range(parts)]

    def second_tasks(h):
        jobs = [call(finish, 1, h)] + [call(forward_unit, 2, j, h) for j in range(parts)]
        jobs += [call(middle, h), call(turn, 0, h), call(turn, 1, h)]
        for j in list(range(1, places)) + [0]:
            jobs += [call(to_pair, j, h), call(to_side, j, h)]
        return jobs

    steps = [(t, p) for h in range(2) for t in range(2) for p in halves(h)]
    lag = 2
    queue = []
    for i in range(len(steps) + lag):
        if i < len(steps):
            relay(*steps[i])
        if i >= lag:
            pass_on(*steps[i - lag])
        if i == half - 1 + lag:
            queue += first_tasks(0)
        if i == 2 * half - 1 + lag:
            queue += second_tasks(0)
        if i == 3 * half - 1 + lag:
            queue += first_tasks(1)
        for _ in range(3):
            if queue:
                queue.pop(0)()
    for p in list(halves(0))[::-1]:
        queue.append(call(go_home, p))
    for job in queue:
        job()
    for job in second_tasks(1):
        job()

    for j in range(1, parts):
        remote(term, term_recv.at[own], term_send, term_sem.at[own],
               {"expert": lax.rem(own + j, parts)}).start()

    stores = []

    def grad_unit(m, j):
        value = matmul(flipped[0, m], rows_of(m // 2, j, 0))
        value = value + matmul(flipped[1, m], rows_of(m // 2, j, 1))
        grads[m, j] = value.astype(jnp.bfloat16)
        store = pltpu.make_async_copy(
            grads.at[m, j], (out_g, out_u, out_d)[m].at[:, pl.ds(j * part, part)], g_sem.at[m, j]
        )
        store.start()
        stores.append(store)

    units = [(m, j) for m in range(3) for j in range(parts)]
    for _ in range(2):
        grad_unit(*units.pop(0))
    for j in range(1, parts):
        arrived(term_recv.at[lax.rem(own + j, parts)], term_sem.at[lax.rem(own + j, parts)])
    term_recv[own] = term[...]
    total = term_recv[0]
    for j in range(1, parts):
        total = total + term_recv[j]
    total_term[...] = total
    home_s[me] = total
    for p in range(1, groups):
        remote(total_term, home_s.at[me], back_send, back_recv.at[p], {"dp": behind(p)}).start()

    order = list(halves(1))[::-1]
    for i, p in enumerate(order):
        for _ in range(-(-len(units) // (len(order) - i))):
            grad_unit(*units.pop(0))
        go_home(p)

    for p in range(1, groups):
        arrived(home.at[ahead(p)], home_recv.at[p])
        arrived(home_s.at[ahead(p)], back_recv.at[p])
    for store in stores:
        store.wait()
    arrived(recv_s.at[pl.ds(0, groups - 1)], scale_send)
    arrived(home.at[pl.ds(0, groups - 1)], home_send)
    arrived(home_s.at[pl.ds(0, groups - 1)], back_send)
    arrived(term_recv.at[pl.ds(0, parts - 1)], term_send)
    for t in range(2):
        arrived(recvs[t].at[0, pl.ds(0, groups - 1)], dp_send.at[t])
        arrived(recvs[t].at[pl.ds(0, places)], pair_fwd.at[t])
        if places > 1:
            arrived(recvs[t].at[pl.ds(0, places - 1)], side_fwd.at[t])
    for j in range(places):
        arrived(pair_send.at[j], pair_send_sem.at[j])
        if j:
            arrived(side_send.at[j], side_send_sem.at[j])


def exchange(send_t, send_u, send_s, w_gate, w_up, w_down, parts):
    groups, cap, part = send_t.shape
    rows = groups * cap
    hid, width = w_gate.shape
    places = parts // 2
    span = rows // 2
    bf, f32 = jnp.bfloat16, jnp.float32
    dma = pltpu.SemaphoreType.DMA
    vmem = pl.BlockSpec(memory_space=pltpu.VMEM)
    hbm = pl.BlockSpec(memory_space=pl.ANY)
    grad = jax.ShapeDtypeStruct((hid, width), bf)
    return pl.pallas_call(
        functools.partial(kernel, groups, parts),
        out_shape=(
            jax.ShapeDtypeStruct((groups, cap, part), bf),
            jax.ShapeDtypeStruct((groups, 2, 8, span), f32),
            grad, grad, grad,
        ),
        in_specs=[vmem] * 3 + [hbm] * 3,
        out_specs=(vmem, vmem, hbm, hbm, hbm),
        scratch_shapes=[
            pltpu.VMEM((parts, groups, cap, part), bf),
            pltpu.VMEM((parts, groups, cap, part), bf),
            pltpu.VMEM((groups, cap, 128), bf),
            pltpu.VMEM((3, parts, hid, part), bf),
            pltpu.VMEM((2, 3, hid, span), f32),
            pltpu.VMEM((2, 3, hid, span), bf),
            pltpu.VMEM((2, 2, span, hid), bf),
            pltpu.VMEM((3, parts, hid, part), bf),
            pltpu.VMEM((2, 8, span), f32),
            pltpu.VMEM((parts, 2, 8, span), f32),
            pltpu.VMEM((2, 8, span), f32),
            pltpu.VMEM((places, groups, cap, part), bf),
            pltpu.VMEM((places, groups, cap, part), bf),
            pltpu.VMEM((places, groups, cap, part), bf),
            pltpu.VMEM((places, groups, cap, part), bf),
            pltpu.VMEM((groups, cap, part), f32),
            pltpu.VMEM((groups, cap, part), bf),
            dma((3, parts)), dma((3, parts)), dma((2,)), dma((2, parts, groups)),
            dma((groups,)), dma((2,)), dma((2,)), dma((2,)), dma,
            dma((places,)), dma((places, 2)), dma((places,)), dma((places, groups)),
            dma, dma((groups,)), dma, dma((parts,)), dma, dma((groups,)),
        ],
        compiler_params=pltpu.CompilerParams(
            collective_id=0, has_side_effects=True, vmem_limit_bytes=62 * 1024 * 1024
        ),
    )(send_t, send_u, send_s, w_gate, w_up, w_down)


def per_device(tokens, upstream, gates, expert_ids, w_gate, w_up, w_down):
    groups = lax.axis_size("dp")
    parts = lax.axis_size("expert")
    experts = groups * w_gate.shape[0]
    tok_rows, width = tokens.shape
    top = expert_ids.shape[1]
    cap = 2 * tok_rows * top // experts
    part = upstream.shape[1]
    rows = experts * cap
    own = lax.axis_index("expert")
    tok_part = lax.dynamic_slice_in_dim(tokens, own * part, part, axis=1)
    flat = expert_ids.reshape(-1)
    count = flat.shape[0]
    earlier = jnp.arange(count)[None, :] < jnp.arange(count)[:, None]
    same = flat[:, None] == flat[None, :]
    position = jnp.sum((earlier & same).astype(jnp.int32), axis=1)
    slot = (flat * cap + position).reshape(tok_rows, top)
    hit = slot[None, :, :] == jnp.arange(rows, dtype=jnp.int32)[:, None, None]
    pick = jnp.sum(hit.astype(jnp.float32), axis=2).astype(jnp.bfloat16)
    scale = jnp.sum(jnp.where(hit, gates.astype(jnp.float32)[None], 0.0), axis=(1, 2))
    send_t = matmul(pick, tok_part).astype(jnp.bfloat16).reshape(groups, cap, part)
    send_u = matmul(pick, upstream).astype(jnp.bfloat16).reshape(groups, cap, part)
    send_s = jnp.broadcast_to(scale[:, None], (rows, 128)).astype(jnp.bfloat16)
    home, home_s, grad_gate, grad_up, grad_down = exchange(
        send_t, send_u, send_s.reshape(groups, cap, 128), w_gate[0], w_up[0], w_down[0], parts
    )
    grad_x = contract_first(pick, home.reshape(rows, part)).astype(jnp.bfloat16)
    half = groups // 2
    odds = [k for k in range(half - 1, 0, -1) if k % 2]
    shifts = [0, half] + odds
    shifts = jnp.array(shifts + [k for k in range(groups) if k not in shifts])
    away = lax.rem(jnp.arange(groups) - lax.axis_index("dp") + groups, groups)
    terms = home_s[:, :, 0, :].reshape(groups, groups, cap)
    mine = (shifts[None, :] == away[:, None])[:, :, None]
    terms = jnp.sum(jnp.where(mine, terms, 0.0), axis=1).reshape(rows)
    grad_gates = jnp.sum(jnp.where(hit, terms[:, None, None], 0.0), axis=0)
    return (grad_x, grad_gates, grad_gate[None], grad_up[None], grad_down[None])


def solution(mesh):
    in_specs = (
        P("dp", None),
        P("dp", "expert"),
        P("dp", None),
        P("dp", None),
        P("dp", "expert", None),
        P("dp", "expert", None),
        P("dp", "expert", None),
    )
    out_specs = (
        P("dp", "expert"),
        P("dp", None),
        P("dp", "expert", None),
        P("dp", "expert", None),
        P("dp", "expert", None),
    )
    return jax.shard_map(
        per_device, mesh=mesh, in_specs=in_specs, out_specs=out_specs, check_vma=False
    )
```

```python
import functools

import jax
import jax.numpy as jnp
from jax import lax
from jax.experimental import pallas as pl
from jax.experimental.pallas import tpu as pltpu
from jax.sharding import PartitionSpec as P

MESH = pltpu.DeviceIdType.MESH if hasattr(pltpu, "DeviceIdType") else pl.DeviceIdType.MESH


def contract_last(left, right):
    return lax.dot_general(
        left, right, (((1,), (1,)), ((), ())), preferred_element_type=jnp.float32
    )


def contract_first(left, right):
    return lax.dot_general(
        left, right, (((0,), (0,)), ((), ())), preferred_element_type=jnp.float32
    )


def matmul(left, right):
    return jnp.dot(left, right, preferred_element_type=jnp.float32)


def kernel(
    groups, parts,
    send_t, send_u, send_s, w_g_hbm, w_u_hbm, w_d_hbm,
    home, home_s, out_g, out_u, out_d,
    recv_t, recv_u, recv_s, weights, pre, flipped, straight, grads,
    term, term_recv, total_term,
    pair_send, pair_recv, side_send, side_recv, own_sum, out_send,
    w_sem, g_sem, local_sem, recv_sem, scale_sem, dp_send, pair_fwd, side_fwd,
    scale_send, pair_send_sem, pair_recv_sem, side_send_sem, side_recv_sem,
    home_send, home_recv, term_send, term_sem, back_send, back_recv,
):
    me, own = lax.axis_index("dp"), lax.axis_index("expert")
    core, place = lax.rem(own, 2), lax.div(own, 2)
    places = parts // 2
    partner = place * 2 + (1 - core)
    cap, part = send_t.shape[1:]
    rows = groups * cap
    hid = weights.shape[2]
    sends, recvs = (send_t, send_u), (recv_t, recv_u)

    paired = groups & (groups - 1) == 0

    def crossed(k):
        spot = me
        for bit in [1 << b for b in range(groups.bit_length()) if k >> b & 1]:
            spot = spot + bit * (1 - 2 * lax.rem(lax.div(me, bit), 2))
        return spot

    def ahead(k):
        return crossed(k) if paired else lax.rem(me + k, groups)

    def behind(k):
        return crossed(k) if paired else lax.rem(me + groups - k, groups)

    def aside(j):
        return lax.rem(place + j, places)

    def remote(src, dst, send_sem, sem, target):
        return pltpu.make_async_remote_copy(
            src_ref=src, dst_ref=dst, send_sem=send_sem, recv_sem=sem,
            device_id=target, device_id_type=MESH,
        )

    def arrived(ref, sem):
        pltpu.make_async_copy(ref, ref, sem).wait()

    loads = []
    for m, w_hbm in enumerate((w_g_hbm, w_u_hbm, w_d_hbm)):
        for j in range(parts):
            load = pltpu.make_async_copy(
                w_hbm.at[:, pl.ds(j * part, part)], weights.at[m, j], w_sem.at[m, j]
            )
            load.start()
            loads.append(load)

    barrier = pltpu.get_barrier_semaphore()
    for k in range(1, groups):
        pl.semaphore_signal(barrier, inc=1, device_id={"dp": ahead(k)}, device_id_type=MESH)
    for j in range(1, parts):
        pl.semaphore_signal(
            barrier, inc=1, device_id={"expert": lax.rem(own + j, parts)}, device_id_type=MESH
        )
    pl.semaphore_wait(barrier, groups + parts - 2)

    for k in range(1, groups):
        to = ahead(k)
        for t in range(2):
            if t == 0:
                remote(send_t.at[to], recv_t.at[own, me], dp_send.at[0],
                       recv_sem.at[0, own, me], {"dp": to}).start()
    for k in range(1, groups):
        to = ahead(k)
        remote(send_s.at[to], recv_s.at[me], scale_send, scale_sem.at[me], {"dp": to}).start()
        remote(send_u.at[to], recv_u.at[own, me], dp_send.at[1],
               recv_sem.at[1, own, me], {"dp": to}).start()
    keeps = []
    for t in range(2):
        keep = pltpu.make_async_copy(sends[t].at[me], recvs[t].at[own, me], local_sem.at[t])
        keep.start()
        keeps.append(keep)
    recv_s[me] = send_s[me]

    def relay(t, k):
        s = behind(k)
        spot = recvs[t].at[own, s]
        if k == 0:
            source = sends[t].at[me]
        else:
            arrived(spot, recv_sem.at[t, own, s])
            source = spot
        for j in range(1, places):
            remote(source, spot, side_fwd.at[t], recv_sem.at[t, own, s],
                   {"expert": aside(j) * 2 + core}).start()
        remote(source, spot, pair_fwd.at[t], recv_sem.at[t, own, s], {"expert": partner}).start()

    def pass_on(t, k):
        s = behind(k)
        for j in range(1, places):
            part_of = aside(j) * 2 + core
            spot = recvs[t].at[part_of, s]
            arrived(spot, recv_sem.at[t, part_of, s])
            remote(spot, spot, pair_fwd.at[t], recv_sem.at[t, part_of, s],
                   {"expert": partner}).start()

    def finish(t):
        keeps[t].wait()
        for k in range(groups):
            s = behind(k)
            for j in range(places):
                part_of = aside(j) * 2 + (1 - core)
                arrived(recvs[t].at[part_of, s], recv_sem.at[t, part_of, s])

    def forward_unit(m, j):
        loads[m * parts + j].wait()
        block = recvs[m // 2][j].reshape(rows, part)
        value = contract_last(weights[m, j], block)
        if j == 0:
            pre[m] = value
        else:
            pre[m] = pre[m] + value

    units = [(m, j) for m in range(2) for j in range(parts)]
    steps = [(t, k) for t in range(2) for k in range(groups)]
    lag = 2
    begin = groups + lag
    for i in range(len(steps) + lag):
        if i < len(steps):
            relay(*steps[i])
        if i >= lag:
            pass_on(*steps[i - lag])
        if i == begin - 1:
            finish(0)
        if i >= begin - 1:
            share = -(-len(units) // max(1, len(steps) + lag - i))
            for _ in range(share):
                if units:
                    forward_unit(*units.pop(0))
    for unit in units:
        forward_unit(*unit)
    finish(1)
    for j in range(parts):
        forward_unit(2, j)

    for k in range(1, groups):
        arrived(recv_s.at[behind(k)], scale_sem.at[behind(k)])
    scale = jnp.transpose(recv_s[...].reshape(rows, 128).astype(jnp.float32))[0:1, :]
    tile = 32
    term[...] = jnp.zeros_like(term)

    @pl.loop(0, hid // tile)
    def _(step):
        at = pl.ds(pl.multiple_of(step * tile, tile), tile)
        gate, up, back = pre[0, at, :], pre[1, at, :], pre[2, at, :]
        sigma = jax.nn.sigmoid(gate)
        swish = gate * sigma
        slope = sigma * (1.0 + gate * (1.0 - sigma))
        act = (swish * up).astype(jnp.bfloat16).astype(jnp.float32)
        term[...] += jnp.broadcast_to(jnp.sum(act * back, axis=0, keepdims=True), term.shape)
        weighted = scale * back
        flipped[0, at, :] = (weighted * up * slope).astype(jnp.bfloat16)
        flipped[1, at, :] = (weighted * swish).astype(jnp.bfloat16)
        flipped[2, at, :] = (scale * act).astype(jnp.bfloat16)

    for j in range(1, parts):
        remote(term, term_recv.at[own], term_send, term_sem.at[own],
               {"expert": lax.rem(own + j, parts)}).start()
    for m in range(2):
        straight[m] = jnp.transpose(flipped[m].astype(jnp.float32)).astype(jnp.bfloat16)

    block_rows = min(rows, 256)

    def piece(which, lo):
        at = pl.ds(lo, block_rows)
        value = matmul(straight[0, at, :], weights[0, which])
        return value + matmul(straight[1, at, :], weights[1, which])

    chunk = block_rows // cap
    for j in list(range(1, places)) + [0]:
        there = aside(j) * 2
        for lo in range(0, rows, block_rows):
            value = piece(there + 1 - core, lo).astype(jnp.bfloat16)
            pair_send[j, pl.ds(lo // cap, chunk)] = value.reshape(chunk, cap, part)
        pair = remote(pair_send.at[j], pair_recv.at[j], pair_send_sem.at[j],
                      pair_recv_sem.at[j], {"expert": partner})
        pair.start()
        for lo in range(0, rows, block_rows):
            value = piece(there + core, lo)
            own_sum[pl.ds(lo // cap, chunk)] = value.reshape(chunk, cap, part)
        pair.wait_recv()
        if j == 0:
            continue
        for k in list(range(1, groups)) + [0]:
            to = ahead(k)
            both = own_sum[to] + pair_recv[j, to].astype(jnp.float32)
            side_send[j, to] = both.astype(jnp.bfloat16)
            remote(side_send.at[j, to], side_recv.at[j, to], side_send_sem.at[j],
                   side_recv_sem.at[j, to], {"expert": there + core}).start()

    stores = []

    def grad_unit(m, j):
        block = recvs[m // 2][j].reshape(rows, part)
        grads[m, j] = matmul(flipped[m], block).astype(jnp.bfloat16)
        store = pltpu.make_async_copy(
            grads.at[m, j], (out_g, out_u, out_d)[m].at[:, pl.ds(j * part, part)], g_sem.at[m, j]
        )
        store.start()
        stores.append(store)

    for j in range(1, parts):
        arrived(term_recv.at[lax.rem(own + j, parts)], term_sem.at[lax.rem(own + j, parts)])
    term_recv[own] = term[...]
    total = term_recv[0]
    for j in range(1, parts):
        total = total + term_recv[j]
    total_term[...] = total
    home_s[me] = total
    for k in range(1, groups):
        remote(total_term, home_s.at[me], back_send, back_recv.at[me], {"dp": ahead(k)}).start()

    units = [(m, j) for m in range(3) for j in range(parts)]
    order = list(range(1, groups)) + [0]
    for i, k in enumerate(order):
        for _ in range(-(-len(units) // (len(order) - i))):
            grad_unit(*units.pop(0))
        to = ahead(k)
        value = own_sum[to] + pair_recv[0, to].astype(jnp.float32)
        for j in range(1, places):
            arrived(side_recv.at[j, to], side_recv_sem.at[j, to])
            value = value + side_recv[j, to].astype(jnp.float32)
        if k == 0:
            home[me] = value.astype(jnp.bfloat16)
        else:
            out_send[to] = value.astype(jnp.bfloat16)
            remote(out_send.at[to], home.at[me], home_send, home_recv.at[me], {"dp": to}).start()

    for k in range(1, groups):
        s = behind(k)
        arrived(home.at[s], home_recv.at[s])
        arrived(home_s.at[s], back_recv.at[s])
    for store in stores:
        store.wait()
    arrived(recv_s.at[pl.ds(0, groups - 1)], scale_send)
    arrived(home.at[pl.ds(0, groups - 1)], home_send)
    arrived(home_s.at[pl.ds(0, groups - 1)], back_send)
    arrived(term_recv.at[pl.ds(0, parts - 1)], term_send)
    for t in range(2):
        arrived(recvs[t].at[0, pl.ds(0, groups - 1)], dp_send.at[t])
        arrived(recvs[t].at[pl.ds(0, places)], pair_fwd.at[t])
        if places > 1:
            arrived(recvs[t].at[pl.ds(0, places - 1)], side_fwd.at[t])
    for j in range(places):
        arrived(pair_send.at[j], pair_send_sem.at[j])
        if j:
            arrived(side_send.at[j], side_send_sem.at[j])


def exchange(send_t, send_u, send_s, w_gate, w_up, w_down, parts):
    groups, cap, part = send_t.shape
    rows = groups * cap
    hid, width = w_gate.shape
    places = parts // 2
    bf, f32 = jnp.bfloat16, jnp.float32
    dma = pltpu.SemaphoreType.DMA
    vmem = pl.BlockSpec(memory_space=pltpu.VMEM)
    hbm = pl.BlockSpec(memory_space=pl.ANY)
    grad = jax.ShapeDtypeStruct((hid, width), bf)
    return pl.pallas_call(
        functools.partial(kernel, groups, parts),
        out_shape=(
            jax.ShapeDtypeStruct((groups, cap, part), bf),
            jax.ShapeDtypeStruct((groups, 8, rows), f32),
            grad, grad, grad,
        ),
        in_specs=[vmem] * 3 + [hbm] * 3,
        out_specs=(vmem, vmem, hbm, hbm, hbm),
        scratch_shapes=[
            pltpu.VMEM((parts, groups, cap, part), bf),
            pltpu.VMEM((parts, groups, cap, part), bf),
            pltpu.VMEM((groups, cap, 128), bf),
            pltpu.VMEM((3, parts, hid, part), bf),
            pltpu.VMEM((3, hid, rows), f32),
            pltpu.VMEM((3, hid, rows), bf),
            pltpu.VMEM((2, rows, hid), bf),
            pltpu.VMEM((3, parts, hid, part), bf),
            pltpu.VMEM((8, rows), f32),
            pltpu.VMEM((parts, 8, rows), f32),
            pltpu.VMEM((8, rows), f32),
            pltpu.VMEM((places, groups, cap, part), bf),
            pltpu.VMEM((places, groups, cap, part), bf),
            pltpu.VMEM((places, groups, cap, part), bf),
            pltpu.VMEM((places, groups, cap, part), bf),
            pltpu.VMEM((groups, cap, part), f32),
            pltpu.VMEM((groups, cap, part), bf),
            dma((3, parts)), dma((3, parts)), dma((2,)), dma((2, parts, groups)),
            dma((groups,)), dma((2,)), dma((2,)), dma((2,)), dma,
            dma((places,)), dma((places,)), dma((places,)), dma((places, groups)),
            dma, dma((groups,)), dma, dma((parts,)), dma, dma((groups,)),
        ],
        compiler_params=pltpu.CompilerParams(
            collective_id=0, has_side_effects=True, vmem_limit_bytes=62 * 1024 * 1024
        ),
    )(send_t, send_u, send_s, w_gate, w_up, w_down)


def per_device(tokens, upstream, gates, expert_ids, w_gate, w_up, w_down):
    groups = lax.axis_size("dp")
    parts = lax.axis_size("expert")
    experts = groups * w_gate.shape[0]
    tok_rows, width = tokens.shape
    top = expert_ids.shape[1]
    cap = 2 * tok_rows * top // experts
    part = upstream.shape[1]
    rows = experts * cap
    own = lax.axis_index("expert")
    tok_part = lax.dynamic_slice_in_dim(tokens, own * part, part, axis=1)
    flat = expert_ids.reshape(-1)
    count = flat.shape[0]
    earlier = jnp.arange(count)[None, :] < jnp.arange(count)[:, None]
    same = flat[:, None] == flat[None, :]
    position = jnp.sum((earlier & same).astype(jnp.int32), axis=1)
    slot = (flat * cap + position).reshape(tok_rows, top)
    hit = slot[None, :, :] == jnp.arange(rows, dtype=jnp.int32)[:, None, None]
    pick = jnp.sum(hit.astype(jnp.float32), axis=2).astype(jnp.bfloat16)
    scale = jnp.sum(jnp.where(hit, gates.astype(jnp.float32)[None], 0.0), axis=(1, 2))
    send_t = matmul(pick, tok_part).astype(jnp.bfloat16).reshape(groups, cap, part)
    send_u = matmul(pick, upstream).astype(jnp.bfloat16).reshape(groups, cap, part)
    send_s = jnp.broadcast_to(scale[:, None], (rows, 128)).astype(jnp.bfloat16)
    home, home_s, grad_gate, grad_up, grad_down = exchange(
        send_t, send_u, send_s.reshape(groups, cap, 128), w_gate[0], w_up[0], w_down[0], parts
    )
    grad_x = contract_first(pick, home.reshape(rows, part)).astype(jnp.bfloat16)
    terms = home_s[:, 0, :].reshape(groups, groups, cap)
    terms = lax.dynamic_index_in_dim(terms, lax.axis_index("dp"), 1, keepdims=False).reshape(rows)
    grad_gates = jnp.sum(jnp.where(hit, terms[:, None, None], 0.0), axis=0)
    return (grad_x, grad_gates, grad_gate[None], grad_up[None], grad_down[None])


def solution(mesh):
    in_specs = (
        P("dp", None),
        P("dp", "expert"),
        P("dp", None),
        P("dp", None),
        P("dp", "expert", None),
        P("dp", "expert", None),
        P("dp", "expert", None),
    )
    out_specs = (
        P("dp", "expert"),
        P("dp", None),
        P("dp", "expert", None),
        P("dp", "expert", None),
        P("dp", "expert", None),
    )
    return jax.shard_map(
        per_device, mesh=mesh, in_specs=in_specs, out_specs=out_specs, check_vma=False
    )
```
